512 devices in a mesh: gx: 32 (over y, x), gy: 16 (over z, core).
Axes of the slice: x: 4, y: 8, z: 8, core: 2. Of those that a mesh axis runs over, the one named last changes fastest.
Arguments:
- source: float32 [512, 256, 128], P('gx', 'gy'), may hold values from -8 to 8
- diffuse_first: float32 [512, 256, 128], P('gx', 'gy'), may hold values from 0.5 to 8
- diffuse_second: float32 [512, 256, 128], P('gx', 'gy'), may hold values from 0.5 to 8
- diffuse_third: float32 [512, 256, 128], P('gx', 'gy'), may hold values from 0.5 to 8
- reaction: float32 [512, 256, 128], P('gx', 'gy'), may hold values from 0.005 to 0.05
- deflation: float32 [8, 512, 256, 128], P(None, 'gx', 'gy'), may hold values from -1.5 to 1.5
Outputs:
- iterate: float32 [512, 256, 128], P('gx', 'gy')
- residual: float32 [512, 256, 128], P('gx', 'gy')
The draws below stay inside these ranges and needn't reach their ends.
All inputs are finite; a program needn't handle non-finite values.
Results may differ from the reference program's by a relative error of at most 0.0003.
Values sent between devices are 32-bit elements; how exact they have to be, the bound alone decides.
A program may use at most 64 MiB of HBM per device.

```python
import math
import jax
import jax.numpy as jnp
from jax import lax

NZ = 128
LEVELS = 3
COARSE_SWEEPS = 3
BASIS = 8
ITERS = 2
NX = 512
NY = 256


def smooth_modes():
    orders = jnp.arange(BASIS, dtype=jnp.int32)
    first_freq = (orders % 2).astype(jnp.float32)
    second_freq = (orders // 2 % 2).astype(jnp.float32)
    third_freq = (orders // 4).astype(jnp.float32)
    first = (jnp.arange(NX, dtype=jnp.float32) + 0.5) / NX
    second = (jnp.arange(NY, dtype=jnp.float32) + 0.5) / NY
    third = (jnp.arange(NZ, dtype=jnp.float32) + 0.5) / NZ
    along_first = jnp.cos(math.pi * first_freq[:, None] * first[None, :])
    along_second = jnp.cos(math.pi * second_freq[:, None] * second[None, :])
    along_third = jnp.cos(math.pi * third_freq[:, None] * third[None, :])
    return along_first[:, :, None, None] * along_second[:, None, :, None] * along_third[:, None, None, :]


def draw_deflation(key, part):
    modes = smooth_modes()
    spread = jax.random.uniform(key, modes.shape, jnp.float32, -1.0, 1.0)
    factor = 1.0 + 0.5 * spread
    return modes * factor


def draw_source(key, part):
    modes = smooth_modes()
    amp_key = jax.random.fold_in(key, 11)
    rough_key = jax.random.fold_in(key, 12)
    amplitudes = 0.05 * jnp.clip(jax.random.normal(amp_key, (BASIS,), jnp.float32), -3.0, 3.0)
    rough = jnp.clip(jax.random.normal(rough_key, (NX, NY, NZ), jnp.float32), -4.0, 4.0)
    return rough + jnp.sum(amplitudes[:, None, None, None] * modes, axis=0)


def shard_levels(rng, dims, split, least, largest):
    gain = 1.0
    for dim, parts in split:
        heights = jax.random.uniform(jax.random.fold_in(jax.random.fold_in(rng, 6), dim), (parts,), jnp.float32, least / len(split), largest / len(split))
        gain = gain * jnp.repeat(jnp.exp(heights), dims[dim] // parts).reshape((-1,) + (1,) * (len(dims) - 1 - dim))
    return gain


def setup_inputs(seed: int = 0) -> dict:
    key_list = jax.random.split(jax.random.key(seed), 7)
    return {
        "source": draw_source(jax.random.fold_in(key_list[6], 71), 0),
        "diffuse_first": jnp.clip(jnp.exp(math.log(8.0) - 2.7725887 * jax.random.uniform(key_list[1], (NX, NY, NZ), jnp.float32) ** shard_levels(key_list[1], (NX, NY, NZ), ((0, 32), (1, 16)), -0.2, 0.2)), 0.5, 8.0),
        "diffuse_second": jnp.clip(jnp.exp(math.log(8.0) - 2.7725887 * jax.random.uniform(key_list[2], (NX, NY, NZ), jnp.float32) ** shard_levels(key_list[2], (NX, NY, NZ), ((0, 32), (1, 16)), -0.2, 0.2)), 0.5, 8.0),
        "diffuse_third": jnp.clip(jnp.exp(math.log(8.0) - 2.7725887 * jax.random.uniform(key_list[3], (NX, NY, NZ), jnp.float32) ** shard_levels(key_list[3], (NX, NY, NZ), ((0, 32), (1, 16)), -0.2, 0.2)), 0.5, 8.0),
        "reaction": jnp.clip(jnp.exp(math.log(0.05) - 2.3025851 * jax.random.uniform(key_list[4], (NX, NY, NZ), jnp.float32) ** shard_levels(key_list[4], (NX, NY, NZ), ((0, 32), (1, 16)), -0.2, 0.2)), 0.005, 0.05),
        "deflation": draw_deflation(jax.random.fold_in(key_list[6], 71), 0),
    }


RELAX_WEIGHT = 0.6
TOP_PRECISION = lax.Precision.HIGHEST

def shift_lower(values, which):
    which = which % values.ndim
    count = values.shape[which]
    zero = jnp.zeros_like(lax.slice_in_dim(values, 0, 1, axis=which))
    return jnp.concatenate([zero, lax.slice_in_dim(values, 0, count - 1, axis=which)], axis=which)

def shift_upper(values, which):
    which = which % values.ndim
    count = values.shape[which]
    zero = jnp.zeros_like(lax.slice_in_dim(values, 0, 1, axis=which))
    return jnp.concatenate([lax.slice_in_dim(values, 1, count, axis=which), zero], axis=which)

def fold_pairs(values, which):
    shape = values.shape
    new_shape = shape[:which] + (shape[which] // 2, 2) + shape[which + 1:]
    return values.reshape(new_shape).sum(axis=which + 1)

def fold_blocks(values, which_dims):
    for which in which_dims:
        values = fold_pairs(values, which)
    return values

def make_level(face_first, lower_first, face_second, lower_second, face_third, lower_third, react):
    diag = react + face_first + lower_first + face_second + lower_second + face_third + lower_third
    return (face_first, lower_first, face_second, lower_second, face_third, lower_third, react, diag, 1.0 / diag)

def coarsen(level):
    face_first, lower_first, face_second, lower_second, face_third, lower_third, react, diag, inverse = level
    return make_level(fold_blocks(face_first[1::2], (1, 2)), fold_blocks(lower_first[0::2], (1, 2)), fold_blocks(face_second[:, 1::2], (0, 2)), fold_blocks(lower_second[:, 0::2], (0, 2)), fold_blocks(face_third[:, :, 1::2], (0, 1)), fold_blocks(lower_third[:, :, 0::2], (0, 1)), fold_blocks(react, (0, 1, 2)))

def operate(field, level):
    face_first, lower_first, face_second, lower_second, face_third, lower_third, react, diag, inverse = level
    return diag * field - face_first * shift_upper(field, 0) - lower_first * shift_lower(field, 0) - face_second * shift_upper(field, 1) - lower_second * shift_lower(field, 1) - face_third * shift_upper(field, 2) - lower_third * shift_lower(field, 2)

def prolong(coarse):
    return jnp.repeat(jnp.repeat(jnp.repeat(coarse, 2, 0), 2, 1), 2, 2)

def vee_cycle(right, levels, level_index):
    level = levels[level_index]
    inverse = level[8]
    field = RELAX_WEIGHT * right * inverse
    if level_index == len(levels) - 1:
        for sweep in range(COARSE_SWEEPS - 1):
            field = field + RELAX_WEIGHT * (right - operate(field, level)) * inverse
        return field
    defect = right - operate(field, level)
    field = field + prolong(vee_cycle(fold_blocks(defect, (0, 1, 2)), levels, level_index + 1))
    return field + RELAX_WEIGHT * (right - operate(field, level)) * inverse

def small_solve(factor, values):
    count = factor.shape[0]
    forward = []
    for place in range(count):
        value = values[place]
        for other in range(place):
            value = value - factor[place, other] * forward[other]
        forward.append(value / factor[place, place])
    backward = [None] * count
    for place in range(count - 1, -1, -1):
        value = forward[place]
        for other in range(place + 1, count):
            value = value - factor[other, place] * backward[other]
        backward[place] = value / factor[place, place]
    return jnp.stack(backward)

def project(vectors, field):
    return jnp.einsum('kxyz,xyz->k', vectors, field, precision=TOP_PRECISION)

def expand(vectors, weights):
    return jnp.einsum('k,kxyz->xyz', weights, vectors, precision=TOP_PRECISION)

def reference(source, diffuse_first, diffuse_second, diffuse_third, reaction, deflation):
    shape = source.shape
    masks = []
    for which in range(3):
        position = lax.broadcasted_iota(jnp.int32, shape, which)
        masks.append((position < shape[which] - 1).astype(jnp.float32))
    face_first = diffuse_first * masks[0]
    face_second = diffuse_second * masks[1]
    face_third = diffuse_third * masks[2]
    level = make_level(face_first, shift_lower(face_first, 0), face_second, shift_lower(face_second, 1), face_third, shift_lower(face_third, 2), reaction)
    levels = [level]
    for level_index in range(LEVELS - 1):
        levels.append(coarsen(levels[-1]))
    images = jnp.stack([operate(deflation[place], level) for place in range(BASIS)])
    matrix = jnp.einsum('kxyz,mxyz->km', deflation, images, precision=TOP_PRECISION)
    matrix = 0.5 * (matrix + matrix.T)
    factor = jnp.linalg.cholesky(matrix)
    start_weights = small_solve(factor, project(deflation, source))
    iterate = expand(deflation, start_weights)
    residual = source - expand(images, start_weights)
    precond = vee_cycle(residual, levels, 0)
    inner_now = jnp.sum(residual * precond)
    weights = small_solve(factor, project(images, precond))
    search = precond - expand(deflation, weights)
    for turn in range(ITERS):
        image = operate(search, level)
        alpha = inner_now / jnp.sum(search * image)
        iterate = iterate + alpha * search
        residual = residual - alpha * image
        if turn + 1 < ITERS:
            precond = vee_cycle(residual, levels, 0)
            inner_next = jnp.sum(residual * precond)
            weights = small_solve(factor, project(images, precond))
            search = precond + inner_next / inner_now * search - expand(deflation, weights)
            inner_now = inner_next
    return (iterate, residual)
```

```python
import functools

import jax
import jax.numpy as jnp
from jax import lax
from jax.experimental import pallas as pl
from jax.experimental.pallas import tpu as pltpu
from jax.sharding import PartitionSpec as P

LEVELS = 3
COARSE_SWEEPS = 3
ITERS = 2
BASIS = 8
RELAX_WEIGHT = 0.6

N = 16
LANES = 128
ROW = 4
SUMS = 2 * ITERS + 1
CYCLES = ITERS
FINE_EXCHANGES = 2 * CYCLES + ITERS
MID_EXCHANGES = 2 * CYCLES
COARSE_EXCHANGES = (COARSE_SWEEPS - 1) * CYCLES
EXCHANGES = (FINE_EXCHANGES, MID_EXCHANGES, COARSE_EXCHANGES)

FF, LF, FS, LS, FT, LT, DIAG, INV = range(8)


def kernel(
    sizes,
    source,
    diffuse_first,
    diffuse_second,
    diffuse_third,
    reaction,
    deflation,
    iterate_out,
    residual_out,
    level0,
    level1,
    level2,
    images,
    search,
    face_send,
    face_recv,
    basis_second_send,
    basis_first_recv,
    basis_second_recv,
    first_send0,
    first_recv0,
    second_send0,
    second_recv0,
    first_send1,
    first_recv1,
    second_send1,
    second_recv1,
    first_send2,
    first_recv2,
    second_send2,
    second_recv2,
    gather_second,
    gather_x,
    gather_y,
    setup_sems,
    halo_sems0,
    halo_sems1,
    halo_sems2,
    sum_sems,
):
    gx_count, gy_count = sizes
    x_count = ROW
    y_count = gx_count // ROW
    gx = lax.axis_index("gx")
    gy = lax.axis_index("gy")
    gx_next, gx_prev = lax.rem(gx + 1, gx_count), lax.rem(gx + gx_count - 1, gx_count)
    gy_next, gy_prev = lax.rem(gy + 1, gy_count), lax.rem(gy + gy_count - 1, gy_count)
    x, y = lax.rem(gx, x_count), gx // x_count

    second_peers = [(gx, lax.rem(gy + d, gy_count)) for d in range(1, gy_count)]
    x_peers = [(y * x_count + lax.rem(x + d, x_count), gy) for d in range(1, x_count)]
    y_peers = [(lax.rem(y + d, y_count) * x_count + x, gy) for d in range(1, y_count)]

    barrier = pltpu.get_barrier_semaphore()
    greeted = second_peers + x_peers + y_peers + [(gx_next, gy), (gx_prev, gy)]
    for peer in greeted:
        pl.semaphore_signal(
            barrier, inc=1, device_id=peer, device_id_type=pl.DeviceIdType.MESH
        )

    def send(src, dst, sems, peer):
        copy = pltpu.make_async_remote_copy(
            src_ref=src,
            dst_ref=dst,
            send_sem=sems[0],
            recv_sem=sems[1],
            device_id=peer,
            device_id_type=pl.DeviceIdType.MESH,
        )
        copy.start()
        return copy

    def iota(shape, dim):
        return lax.broadcasted_iota(jnp.int32, shape, dim)

    def roll(values, shift, axis):
        return pltpu.roll(values, shift, axis)

    levels = (level0, level1, level2)
    halo_refs = (
        (first_send0, first_recv0, second_send0, second_recv0, halo_sems0),
        (first_send1, first_recv1, second_send1, second_recv1, halo_sems1),
        (first_send2, first_recv2, second_send2, second_recv2, halo_sems2),
    )
    used = [0, 0, 0]

    shape = (N, N, LANES)
    last_first = (iota(shape, 0) == N - 1) & (gx == gx_count - 1)
    last_second = (iota(shape, 1) == N - 1) & (gy == gy_count - 1)
    last_third = iota(shape, 2) == LANES - 1
    face_first = jnp.where(last_first, 0.0, diffuse_first[...])
    face_second = jnp.where(last_second, 0.0, diffuse_second[...])
    face_third = jnp.where(last_third, 0.0, diffuse_third[...])
    level0[FF] = face_first
    level0[FS] = face_second
    level0[FT] = face_third
    level0[LT] = roll(face_third, 1, 2)
    face_send[0] = face_first[N - 1]
    face_send[1] = face_second[:, N - 1, :]
    basis = deflation[...]
    basis_second_send[0] = basis[:, :, 0, :]
    basis_second_send[1] = basis[:, :, N - 1, :]

    pl.semaphore_wait(barrier, len(greeted))

    def setup_pair(place):
        return setup_sems.at[0, place], setup_sems.at[1, place]

    setup_copies = [
        send(face_send.at[0], face_recv.at[0], setup_pair(0), (gx_next, gy)),
        send(face_send.at[1], face_recv.at[1], setup_pair(1), (gx, gy_next)),
        send(basis_second_send.at[0], basis_second_recv.at[1], setup_pair(2), (gx, gy_prev)),
        send(basis_second_send.at[1], basis_second_recv.at[0], setup_pair(3), (gx, gy_next)),
        send(deflation.at[:, 0], basis_first_recv.at[1], setup_pair(4), (gx_prev, gy)),
        send(deflation.at[:, N - 1], basis_first_recv.at[0], setup_pair(5), (gx_next, gy)),
    ]
    setup_copies[0].wait()
    setup_copies[1].wait()
    row0 = iota(shape, 1)
    lower_first = jnp.concatenate([face_recv[0][None], face_first[: N - 1]], axis=0)
    lower_second = jnp.where(row0 == 0, face_recv[1][:, None, :], roll(face_second, 1, 1))
    level0[LF] = lower_first
    level0[LS] = lower_second

    def finish_level(level, react):
        diag = react + level[FF] + level[LF] + level[FS] + level[LS] + level[FT] + level[LT]
        level[DIAG] = diag
        level[INV] = 1.0 / diag

    finish_level(level0, reaction[...])

    def partner_up(values, step, axis):
        return roll(values, values.shape[axis] - step, axis)

    def halves(values, step, axis):
        even = lax.rem(iota(values.shape, axis) // step, 2) == 0
        return (
            jnp.where(even, values, roll(values, step, axis)),
            jnp.where(even, partner_up(values, step, axis), values),
        )

    def fold(values, step, axis):
        if axis == 0:
            pairs = values.reshape((values.shape[0] // 2, 2) + values.shape[1:])
            return pairs[:, 0] + pairs[:, 1]
        even, odd = halves(values, step, axis)
        return even + odd

    def first_half(values, which):
        pairs = values.reshape((values.shape[0] // 2, 2) + values.shape[1:])
        return pairs[:, which]

    def fold_block(values, step):
        return fold(fold(fold(values, step, 0), step, 1), step, 2)

    def coarsen(fine, coarse, react, step):
        coarse[FF] = fold(fold(first_half(fine[FF], 1), step, 1), step, 2)
        coarse[LF] = fold(fold(first_half(fine[LF], 0), step, 1), step, 2)
        coarse[FS] = halves(fold(fold(fine[FS], step, 0), step, 2), step, 1)[1]
        coarse[LS] = halves(fold(fold(fine[LS], step, 0), step, 2), step, 1)[0]
        coarse[FT] = halves(fold(fold(fine[FT], step, 0), step, 1), step, 2)[1]
        coarse[LT] = halves(fold(fold(fine[LT], step, 0), step, 1), step, 2)[0]
        react = fold_block(react, step)
        finish_level(coarse, react)
        return react

    react1 = coarsen(level0, level1, reaction[...], 1)
    coarsen(level1, level2, react1, 2)

    def inner_part(field, level, step):
        return (
            level[DIAG] * field
            - level[FT] * partner_up(field, step, 2)
            - level[LT] * roll(field, step, 2)
        )

    def outer_part(partial, field, level, step, first_lo, first_hi, second_lo, second_hi):
        row = iota(field.shape, 1)
        upper = jnp.where(row >= N - step, second_hi[:, None, :], partner_up(field, step, 1))
        lower = jnp.where(row < step, second_lo[:, None, :], roll(field, step, 1))
        if field.shape[0] > 1:
            after = jnp.concatenate([field[1:], first_hi[None]], axis=0)
            before = jnp.concatenate([first_lo[None], field[:-1]], axis=0)
        return (
            partial
            - level[FF] * after
            - level[LF] * before
            - level[FS] * upper
            - level[LS] * lower
        )

    def operate(field, which):
        level = levels[which]
        step = 2**which
        first_send, first_recv, second_send, second_recv, sems = halo_refs[which]
        use = used[which]
        used[which] += 1
        cells = field.shape[0]
        first_send[use, 0] = field[0]
        first_send[use, 1] = field[cells - 1]
        second_send[use, 0] = field[:, 0, :]
        second_send[use, 1] = field[:, N - 1, :]

        def pair(place):
            return sems.at[0, use, place], sems.at[1, use, place]

        copies = [
            send(first_send.at[use, 0], first_recv.at[use, 1], pair(0), (gx_prev, gy)),
            send(first_send.at[use, 1], first_recv.at[use, 0], pair(1), (gx_next, gy)),
            send(second_send.at[use, 0], second_recv.at[use, 1], pair(2), (gx, gy_prev)),
            send(second_send.at[use, 1], second_recv.at[use, 0], pair(3), (gx, gy_next)),
        ]
        partial = inner_part(field, level, step)
        for copy in copies:
            copy.wait()
        return outer_part(
            partial,
            field,
            level,
            step,
            first_recv[use, 0],
            first_recv[use, 1],
            second_recv[use, 0],
            second_recv[use, 1],
        )

    def prolong_first(values):
        cells = values.shape[0]
        pairs = jnp.broadcast_to(values[:, None], (cells, 2) + values.shape[1:])
        return pairs.reshape((2 * cells,) + values.shape[1:])

    def cycle(right, which):
        level = levels[which]
        field = RELAX_WEIGHT * right * level[INV]
        if which == LEVELS - 1:
            for _ in range(COARSE_SWEEPS - 1):
                field = field + RELAX_WEIGHT * (right - operate(field, which)) * level[INV]
            return field
        defect = right - operate(field, which)
        field = field + prolong_first(cycle(fold_block(defect, 2**which), which + 1))
        return field + RELAX_WEIGHT * (right - operate(field, which)) * level[INV]

    summed = [0]

    def sum_devices(tile):
        use = summed[0]
        summed[0] += 1
        place = 0
        for buffer, peers, mine in (
            (gather_second, second_peers, gy),
            (gather_x, x_peers, x),
            (gather_y, y_peers, y),
        ):
            slot = buffer.at[use, mine]
            slot[...] = tile
            copies = []
            for peer in peers:
                sems = sum_sems.at[0, use, place], sum_sems.at[1, use, place]
                copies.append(send(slot, slot, sems, peer))
                place += 1
            for copy in copies:
                copy.wait()
            tile = jnp.sum(buffer[use], axis=0)
        return tile

    tile_shape = (8, LANES)
    lane = iota(tile_shape, 1)
    sub = iota(tile_shape, 0)

    def total(values):
        part = jnp.sum(values, axis=0)
        part = part[:8] + part[8:]
        part = jnp.sum(part, axis=0, keepdims=True)
        return jnp.broadcast_to(jnp.sum(part, axis=1, keepdims=True), tile_shape)

    def project(vectors, field):
        gathered = jnp.zeros(tile_shape, jnp.float32)
        for i in range(BASIS):
            part = jnp.sum(vectors[i] * field, axis=0)
            part = jnp.sum(part[:8] + part[8:], axis=0, keepdims=True)
            gathered = jnp.where(sub == i, part, gathered)
        return jnp.broadcast_to(jnp.sum(gathered, axis=1, keepdims=True), tile_shape)

    for copy in setup_copies[2:]:
        copy.wait()

    def image_step(j, tile):
        vector = deflation[j]
        image = outer_part(
            inner_part(vector, level0, 1),
            vector,
            level0,
            1,
            basis_first_recv[0, j],
            basis_first_recv[1, j],
            basis_second_recv[0, j],
            basis_second_recv[1, j],
        )
        images[j] = image
        return jnp.where(lane == j, project(deflation, image), tile)

    tile = lax.fori_loop(0, BASIS, image_step, jnp.zeros(tile_shape, jnp.float32))
    tile = jnp.where(lane == BASIS, project(deflation, source[...]), tile)
    tile = sum_devices(tile)

    def column(values, place):
        return jnp.sum(jnp.where(lane == place, values, 0.0), axis=1, keepdims=True)

    flipped = jnp.zeros(tile_shape, jnp.float32)
    for i in range(BASIS):
        col = column(tile, i)
        turned = jnp.sum(jnp.where(lane == sub, col, 0.0), axis=0, keepdims=True)
        flipped = jnp.where(sub == i, turned, flipped)
    projections = column(tile, BASIS)
    work = jnp.where(lane < BASIS, 0.5 * (tile + flipped), 0.0)
    work = jnp.where(lane - 2 * BASIS == sub, 1.0, work)
    for k in range(BASIS):
        col = column(work, k)
        pivot = col[k : k + 1]
        scaled = work[k : k + 1] / pivot
        work = jnp.where(sub == k, scaled, work - col * scaled)
    inverse_columns = [column(work, 2 * BASIS + i) for i in range(BASIS)]

    def solve(values):
        return [
            jnp.sum(
                jnp.broadcast_to(inverse_columns[i], tile_shape) * values,
                axis=0,
                keepdims=True,
            )[None]
            for i in range(BASIS)
        ]

    def expand(vectors, weights):
        out = weights[0] * vectors[0]
        for i in range(1, BASIS):
            out = out + weights[i] * vectors[i]
        return out

    weights = solve(jnp.broadcast_to(projections, tile_shape))
    iterate_out[...] = expand(deflation, weights)
    residual_out[...] = source[...] - expand(images, weights)

    def precondition():
        residual = residual_out[...]
        precond = cycle(residual, 0)
        sums = jnp.where(
            lane < 64, project(images, precond), total(residual * precond)
        )
        sums = sum_devices(sums)
        turned = roll(sums, 64, 1)
        inner = jnp.where(lane < 64, turned, sums)
        return precond, inner, solve(jnp.where(lane < 64, sums, turned))

    precond, inner_now, weights = precondition()
    search[...] = precond - expand(deflation, weights)
    for turn in range(ITERS):
        direction = search[...]
        image = operate(direction, 0)
        alpha = (inner_now / sum_devices(total(direction * image)))[:1][None]
        iterate_out[...] = iterate_out[...] + alpha * direction
        residual_out[...] = residual_out[...] - alpha * image
        if turn + 1 < ITERS:
            precond, inner_next, weights = precondition()
            ratio = (inner_next / inner_now)[:1][None]
            search[...] = precond + ratio * search[...] - expand(deflation, weights)
            inner_now = inner_next


def per_device(sizes, *args):
    gx_count, gy_count = sizes
    vmem = lambda *shape: pltpu.VMEM(shape, jnp.float32)
    scratch = [
        vmem(8, N, N, LANES),
        vmem(8, N // 2, N, LANES),
        vmem(8, N // 4, N, LANES),
        vmem(BASIS, N, N, LANES),
        vmem(N, N, LANES),
        vmem(2, N, LANES),
        vmem(2, N, LANES),
        vmem(2, BASIS, N, LANES),
        vmem(2, BASIS, N, LANES),
        vmem(2, BASIS, N, LANES),
    ]
    for which, count in enumerate(EXCHANGES):
        scratch += [vmem(count, 2, N, LANES)] * 2 + [vmem(count, 2, N // 2**which, LANES)] * 2
    peers = gy_count - 1 + ROW - 1 + gx_count // ROW - 1
    scratch += [
        vmem(SUMS, gy_count, 8, LANES),
        vmem(SUMS, ROW, 8, LANES),
        vmem(SUMS, gx_count // ROW, 8, LANES),
        pltpu.SemaphoreType.DMA((2, 6)),
        pltpu.SemaphoreType.DMA((2, FINE_EXCHANGES, 4)),
        pltpu.SemaphoreType.DMA((2, MID_EXCHANGES, 4)),
        pltpu.SemaphoreType.DMA((2, COARSE_EXCHANGES, 4)),
        pltpu.SemaphoreType.DMA((2, SUMS, peers)),
    ]
    block = jax.ShapeDtypeStruct((N, N, LANES), jnp.float32)
    return pl.pallas_call(
        functools.partial(kernel, sizes),
        out_shape=(block, block),
        in_specs=[pl.BlockSpec(memory_space=pltpu.VMEM)] * 6,
        out_specs=(pl.BlockSpec(memory_space=pltpu.VMEM),) * 2,
        scratch_shapes=scratch,
        compiler_params=pltpu.CompilerParams(
            collective_id=0, has_side_effects=True, vmem_limit_bytes=48 * 1024 * 1024
        ),
        name="deflated_cg",
    )(*args)


def solution(mesh):
    sizes = (mesh.shape["gx"], mesh.shape["gy"])
    field = P("gx", "gy", None)
    return jax.shard_map(
        functools.partial(per_device, sizes),
        mesh=mesh,
        in_specs=(field, field, field, field, field, P(None, "gx", "gy", None)),
        out_specs=(field, field),
        check_vma=False,
    )
```

```python
import functools

import jax
import jax.numpy as jnp
from jax import lax
from jax.experimental import pallas as pl
from jax.experimental.pallas import tpu as pltpu
from jax.sharding import PartitionSpec as P

LEVELS = 3
COARSE_SWEEPS = 3
ITERS = 2
BASIS = 8
RELAX_WEIGHT = 0.6

N = 16
LANES = 128
SUMS = ITERS + 1
CYCLES = ITERS
FINE_EXCHANGES = 2 * CYCLES + ITERS
MID_EXCHANGES = 2 * CYCLES
COARSE_EXCHANGES = (COARSE_SWEEPS - 1) * CYCLES
EXCHANGES = (FINE_EXCHANGES, MID_EXCHANGES, COARSE_EXCHANGES)

FF, LF, FS, LS, FT, LT, DIAG, INV = range(8)


def kernel(
    sizes,
    source,
    diffuse_first,
    diffuse_second,
    diffuse_third,
    reaction,
    deflation,
    iterate_out,
    residual_out,
    level0,
    level1,
    level2,
    images,
    search,
    image_kept,
    face_send,
    face_recv,
    basis_second_send,
    basis_first_recv,
    basis_second_recv,
    first_send0,
    first_recv0,
    second_send0,
    second_recv0,
    first_send1,
    first_recv1,
    second_send1,
    second_recv1,
    first_send2,
    first_recv2,
    second_send2,
    second_recv2,
    gather_second,
    gather_first,
    setup_sems,
    halo_sems0,
    halo_sems1,
    halo_sems2,
    sum_sems,
):
    gx_count, gy_count = sizes
    gx = lax.axis_index("gx")
    gy = lax.axis_index("gy")
    gx_next, gx_prev = lax.rem(gx + 1, gx_count), lax.rem(gx + gx_count - 1, gx_count)
    gy_next, gy_prev = lax.rem(gy + 1, gy_count), lax.rem(gy + gy_count - 1, gy_count)

    second_peers = [(gx, lax.rem(gy + d, gy_count)) for d in range(1, gy_count)]
    first_peers = [(lax.rem(gx + d, gx_count), gy) for d in range(1, gx_count)]

    barrier = pltpu.get_barrier_semaphore()
    greeted = second_peers + first_peers
    for peer in greeted:
        pl.semaphore_signal(
            barrier, inc=1, device_id=peer, device_id_type=pl.DeviceIdType.MESH
        )

    def send(src, dst, sems, peer):
        copy = pltpu.make_async_remote_copy(
            src_ref=src,
            dst_ref=dst,
            send_sem=sems[0],
            recv_sem=sems[1],
            device_id=peer,
            device_id_type=pl.DeviceIdType.MESH,
        )
        copy.start()
        return copy

    def iota(shape, dim):
        return lax.broadcasted_iota(jnp.int32, shape, dim)

    def roll(values, shift, axis):
        return pltpu.roll(values, shift, axis)

    levels = (level0, level1, level2)
    halo_refs = (
        (first_send0, first_recv0, second_send0, second_recv0, halo_sems0),
        (first_send1, first_recv1, second_send1, second_recv1, halo_sems1),
        (first_send2, first_recv2, second_send2, second_recv2, halo_sems2),
    )
    used = [0, 0, 0]

    shape = (N, N, LANES)
    last_first = (iota(shape, 0) == N - 1) & (gx == gx_count - 1)
    last_second = (iota(shape, 1) == N - 1) & (gy == gy_count - 1)
    last_third = iota(shape, 2) == LANES - 1
    face_first = jnp.where(last_first, 0.0, diffuse_first[...])
    face_second = jnp.where(last_second, 0.0, diffuse_second[...])
    face_third = jnp.where(last_third, 0.0, diffuse_third[...])
    level0[FF] = face_first
    level0[FS] = face_second
    level0[FT] = face_third
    level0[LT] = roll(face_third, 1, 2)
    face_send[0] = face_first[N - 1]
    face_send[1] = face_second[:, N - 1, :]
    basis = deflation[...]
    basis_second_send[0] = basis[:, :, 0, :]
    basis_second_send[1] = basis[:, :, N - 1, :]

    pl.semaphore_wait(barrier, len(greeted))

    def setup_pair(place):
        return setup_sems.at[0, place], setup_sems.at[1, place]

    setup_copies = [
        send(face_send.at[0], face_recv.at[0], setup_pair(0), (gx_next, gy)),
        send(face_send.at[1], face_recv.at[1], setup_pair(1), (gx, gy_next)),
        send(basis_second_send.at[0], basis_second_recv.at[1], setup_pair(2), (gx, gy_prev)),
        send(basis_second_send.at[1], basis_second_recv.at[0], setup_pair(3), (gx, gy_next)),
        send(deflation.at[:, 0], basis_first_recv.at[1], setup_pair(4), (gx_prev, gy)),
        send(deflation.at[:, N - 1], basis_first_recv.at[0], setup_pair(5), (gx_next, gy)),
    ]
    setup_copies[0].wait()
    setup_copies[1].wait()
    row0 = iota(shape, 1)
    lower_first = jnp.concatenate([face_recv[0][None], face_first[: N - 1]], axis=0)
    lower_second = jnp.where(row0 == 0, face_recv[1][:, None, :], roll(face_second, 1, 1))
    level0[LF] = lower_first
    level0[LS] = lower_second

    def finish_level(level, react):
        diag = react + level[FF] + level[LF] + level[FS] + level[LS] + level[FT] + level[LT]
        level[DIAG] = diag
        level[INV] = 1.0 / diag

    finish_level(level0, reaction[...])

    def partner_up(values, step, axis):
        return roll(values, values.shape[axis] - step, axis)

    def halves(values, step, axis):
        even = lax.rem(iota(values.shape, axis) // step, 2) == 0
        return (
            jnp.where(even, values, roll(values, step, axis)),
            jnp.where(even, partner_up(values, step, axis), values),
        )

    def fold(values, step, axis):
        if axis == 0:
            pairs = values.reshape((values.shape[0] // 2, 2) + values.shape[1:])
            return pairs[:, 0] + pairs[:, 1]
        even, odd = halves(values, step, axis)
        return even + odd

    def first_half(values, which):
        pairs = values.reshape((values.shape[0] // 2, 2) + values.shape[1:])
        return pairs[:, which]

    def fold_block(values, step):
        return fold(fold(fold(values, step, 0), step, 1), step, 2)

    def coarsen(fine, coarse, react, step):
        coarse[FF] = fold(fold(first_half(fine[FF], 1), step, 1), step, 2)
        coarse[LF] = fold(fold(first_half(fine[LF], 0), step, 1), step, 2)
        coarse[FS] = halves(fold(fold(fine[FS], step, 0), step, 2), step, 1)[1]
        coarse[LS] = halves(fold(fold(fine[LS], step, 0), step, 2), step, 1)[0]
        coarse[FT] = halves(fold(fold(fine[FT], step, 0), step, 1), step, 2)[1]
        coarse[LT] = halves(fold(fold(fine[LT], step, 0), step, 1), step, 2)[0]
        react = fold_block(react, step)
        finish_level(coarse, react)
        return react

    react1 = coarsen(level0, level1, reaction[...], 1)
    coarsen(level1, level2, react1, 2)

    def inner_part(field, level, step):
        return (
            level[DIAG] * field
            - level[FT] * partner_up(field, step, 2)
            - level[LT] * roll(field, step, 2)
        )

    def outer_part(partial, field, level, step, first_lo, first_hi, second_lo, second_hi):
        row = iota(field.shape, 1)
        upper = jnp.where(row >= N - step, second_hi[:, None, :], partner_up(field, step, 1))
        lower = jnp.where(row < step, second_lo[:, None, :], roll(field, step, 1))
        if field.shape[0] > 1:
            after = jnp.concatenate([field[1:], first_hi[None]], axis=0)
            before = jnp.concatenate([first_lo[None], field[:-1]], axis=0)
        return (
            partial
            - level[FF] * after
            - level[LF] * before
            - level[FS] * upper
            - level[LS] * lower
        )

    def operate(field, which, meanwhile=lambda: None):
        level = levels[which]
        step = 2**which
        first_send, first_recv, second_send, second_recv, sems = halo_refs[which]
        use = used[which]
        used[which] += 1
        cells = field.shape[0]
        first_send[use, 0] = field[0]
        first_send[use, 1] = field[cells - 1]
        second_send[use, 0] = field[:, 0, :]
        second_send[use, 1] = field[:, N - 1, :]

        def pair(place):
            return sems.at[0, use, place], sems.at[1, use, place]

        copies = [
            send(first_send.at[use, 0], first_recv.at[use, 1], pair(0), (gx_prev, gy)),
            send(first_send.at[use, 1], first_recv.at[use, 0], pair(1), (gx_next, gy)),
            send(second_send.at[use, 0], second_recv.at[use, 1], pair(2), (gx, gy_prev)),
            send(second_send.at[use, 1], second_recv.at[use, 0], pair(3), (gx, gy_next)),
        ]
        partial = inner_part(field, level, step)
        meanwhile()
        for copy in copies:
            copy.wait()
        return outer_part(
            partial,
            field,
            level,
            step,
            first_recv[use, 0],
            first_recv[use, 1],
            second_recv[use, 0],
            second_recv[use, 1],
        )

    def prolong_first(values):
        cells = values.shape[0]
        pairs = jnp.broadcast_to(values[:, None], (cells, 2) + values.shape[1:])
        return pairs.reshape((2 * cells,) + values.shape[1:])

    def cycle(right, which):
        level = levels[which]
        field = RELAX_WEIGHT * right * level[INV]
        if which == LEVELS - 1:
            for _ in range(COARSE_SWEEPS - 1):
                field = field + RELAX_WEIGHT * (right - operate(field, which)) * level[INV]
            return field
        defect = right - operate(field, which)
        field = field + prolong_first(cycle(fold_block(defect, 2**which), which + 1))
        return field + RELAX_WEIGHT * (right - operate(field, which)) * level[INV]

    summed = [0]

    def sum_devices(row):
        use = summed[0]
        summed[0] += 1
        place = 0
        for buffer, peers, mine in (
            (gather_second, second_peers, gy),
            (gather_first, first_peers, gx),
        ):
            slot = buffer.at[use, mine]
            slot[...] = row
            copies = []
            for peer in peers:
                sems = sum_sems.at[0, use, place], sum_sems.at[1, use, place]
                copies.append(send(slot, slot, sems, peer))
                place += 1
            for copy in copies:
                copy.wait()
            row = jnp.sum(buffer[use], axis=0)
        return row

    tile_shape = (8, LANES)
    lane = iota(tile_shape, 1)
    sub = iota(tile_shape, 0)

    def parts(fields):
        gathered = jnp.zeros(tile_shape, jnp.float32)
        for i, field in enumerate(fields):
            part = jnp.sum(field, axis=0)
            part = jnp.sum(part[:8] + part[8:], axis=0, keepdims=True)
            gathered = jnp.where(sub == i, part, gathered)
        return jnp.sum(gathered, axis=1, keepdims=True)

    def project(vectors, field):
        return parts(vectors[i] * field for i in range(BASIS))

    def pick(row, places):
        return jnp.sum(jnp.where(lane == places, row, 0.0), axis=1, keepdims=True)

    for copy in setup_copies[2:]:
        copy.wait()

    def image_step(j, tile):
        vector = deflation[j]
        image = outer_part(
            inner_part(vector, level0, 1),
            vector,
            level0,
            1,
            basis_first_recv[0, j],
            basis_first_recv[1, j],
            basis_second_recv[0, j],
            basis_second_recv[1, j],
        )
        images[j] = image
        return jnp.where(lane == j * BASIS + sub, project(deflation, image), tile)

    tile = lax.fori_loop(0, BASIS, image_step, jnp.zeros(tile_shape, jnp.float32))
    tile = jnp.where(
        lane == BASIS * BASIS + sub, project(deflation, source[...]), tile
    )
    row = sum_devices(jnp.sum(tile, axis=0, keepdims=True))

    def column(values, place):
        return jnp.sum(jnp.where(lane == place, values, 0.0), axis=1, keepdims=True)

    projections = pick(row, BASIS * BASIS + sub)
    work = jnp.where(lane - 2 * BASIS == sub, 1.0, 0.0)
    for j in range(BASIS):
        both = 0.5 * (pick(row, BASIS * j + sub) + pick(row, BASIS * sub + j))
        work = jnp.where(lane == j, both, work)
    for k in range(BASIS):
        col = column(work, k)
        pivot = col[k : k + 1]
        scaled = work[k : k + 1] / pivot
        work = jnp.where(sub == k, scaled, work - col * scaled)
    inverse_columns = [column(work, 2 * BASIS + i) for i in range(BASIS)]

    def solve(values):
        return [
            jnp.sum(
                jnp.broadcast_to(inverse_columns[i], tile_shape) * values,
                axis=0,
                keepdims=True,
            )[None]
            for i in range(BASIS)
        ]

    def expand(vectors, weights):
        out = weights[0] * vectors[0]
        for i in range(1, BASIS):
            out = out + weights[i] * vectors[i]
        return out

    weights = solve(jnp.broadcast_to(projections, tile_shape))
    iterate_out[...] = expand(deflation, weights)
    residual_out[...] = source[...] - expand(images, weights)

    inner_now = curve = None
    for turn in range(ITERS):
        residual = residual_out[...]
        precond = cycle(residual, 0)
        held = []

        def products():
            held.append(project(images, precond))
            held.append(residual * precond)
            if turn > 0:
                held.append(precond * image_kept[...])

        image = operate(precond, 0, products)
        scalars = parts([precond * image] + held[1:])
        tile = jnp.where(lane == sub, held[0], 0.0)
        tile = jnp.where(lane == BASIS + sub, scalars, tile)
        row = sum_devices(jnp.sum(tile, axis=0, keepdims=True))
        projected = jnp.broadcast_to(pick(row, sub), tile_shape)
        curve_next, inner_next, cross = [
            jnp.broadcast_to(pick(row, BASIS + i)[:1], (1, LANES))[None] for i in range(3)
        ]
        weights = solve(projected)
        for i in range(BASIS):
            curve_next = curve_next - weights[i] * projected[i : i + 1][None]
        direction = precond - expand(deflation, weights)
        image = image - expand(images, weights)
        if turn > 0:
            ratio = inner_next / inner_now
            direction = direction + ratio * search[...]
            image = image + ratio * image_kept[...]
            curve_next = curve_next + ratio * (ratio * curve + 2.0 * cross)
        inner_now, curve = inner_next, curve_next
        alpha = inner_now / curve
        iterate_out[...] = iterate_out[...] + alpha * direction
        residual_out[...] = residual_out[...] - alpha * image
        if turn + 1 < ITERS:
            search[...] = direction
            image_kept[...] = image


def per_device(sizes, *args):
    gx_count, gy_count = sizes
    vmem = lambda *shape: pltpu.VMEM(shape, jnp.float32)
    scratch = [
        vmem(8, N, N, LANES),
        vmem(8, N // 2, N, LANES),
        vmem(8, N // 4, N, LANES),
        vmem(BASIS, N, N, LANES),
        vmem(N, N, LANES),
        vmem(N, N, LANES),
        vmem(2, N, LANES),
        vmem(2, N, LANES),
        vmem(2, BASIS, N, LANES),
        vmem(2, BASIS, N, LANES),
        vmem(2, BASIS, N, LANES),
    ]
    for which, count in enumerate(EXCHANGES):
        scratch += [vmem(count, 2, N, LANES)] * 2 + [vmem(count, 2, N // 2**which, LANES)] * 2
    peers = gy_count - 1 + gx_count - 1
    scratch += [
        vmem(SUMS, gy_count, 1, LANES),
        vmem(SUMS, gx_count, 1, LANES),
        pltpu.SemaphoreType.DMA((2, 6)),
        pltpu.SemaphoreType.DMA((2, FINE_EXCHANGES, 4)),
        pltpu.SemaphoreType.DMA((2, MID_EXCHANGES, 4)),
        pltpu.SemaphoreType.DMA((2, COARSE_EXCHANGES, 4)),
        pltpu.SemaphoreType.DMA((2, SUMS, peers)),
    ]
    block = jax.ShapeDtypeStruct((N, N, LANES), jnp.float32)
    return pl.pallas_call(
        functools.partial(kernel, sizes),
        out_shape=(block, block),
        in_specs=[pl.BlockSpec(memory_space=pltpu.VMEM)] * 6,
        out_specs=(pl.BlockSpec(memory_space=pltpu.VMEM),) * 2,
        scratch_shapes=scratch,
        compiler_params=pltpu.CompilerParams(
            collective_id=0, has_side_effects=True, vmem_limit_bytes=48 * 1024 * 1024
        ),
        name="deflated_cg",
    )(*args)


def solution(mesh):
    sizes = (mesh.shape["gx"], mesh.shape["gy"])
    field = P("gx", "gy", None)
    return jax.shard_map(
        functools.partial(per_device, sizes),
        mesh=mesh,
        in_specs=(field, field, field, field, field, P(None, "gx", "gy", None)),
        out_specs=(field, field),
        check_vma=False,
    )
```

```python
import functools

import jax
import jax.numpy as jnp
from jax import lax
from jax.experimental import pallas as pl
from jax.experimental.pallas import tpu as pltpu
from jax.sharding import PartitionSpec as P

LEVELS = 3
COARSE_SWEEPS = 3
ITERS = 2
BASIS = 8
RELAX_WEIGHT = 0.6

N = 16
LANES = 128
SUMS = ITERS + 1
CYCLES = ITERS
FINE_EXCHANGES = 2 * CYCLES + ITERS
MID_EXCHANGES = 2 * CYCLES
COARSE_EXCHANGES = (COARSE_SWEEPS - 1) * CYCLES
EXCHANGES = (FINE_EXCHANGES, MID_EXCHANGES, COARSE_EXCHANGES)

FF, LF, FS, LS, FT, LT, DIAG, INV = range(8)


def kernel(
    sizes,
    source,
    diffuse_first,
    diffuse_second,
    diffuse_third,
    reaction,
    deflation,
    iterate_out,
    residual_out,
    level0,
    level1,
    level2,
    images,
    search,
    image_kept,
    face_send,
    face_recv,
    basis_second_send,
    basis_first_recv,
    basis_second_recv,
    first_send0,
    first_recv0,
    second_send0,
    second_recv0,
    first_send1,
    first_recv1,
    second_send1,
    second_recv1,
    first_send2,
    first_recv2,
    second_send2,
    second_recv2,
    gather_second,
    gather_first,
    setup_sems,
    halo_sems0,
    halo_sems1,
    halo_sems2,
    sum_sems,
):
    gx_count, gy_count = sizes
    gx = lax.axis_index("gx")
    gy = lax.axis_index("gy")
    gx_next, gx_prev = lax.rem(gx + 1, gx_count), lax.rem(gx + gx_count - 1, gx_count)
    gy_next, gy_prev = lax.rem(gy + 1, gy_count), lax.rem(gy + gy_count - 1, gy_count)

    second_peers = [(gx, lax.rem(gy + d, gy_count)) for d in range(1, gy_count)]
    first_peers = [(lax.rem(gx + d, gx_count), gy) for d in range(1, gx_count)]

    barrier = pltpu.get_barrier_semaphore()
    greeted = second_peers + first_peers
    for peer in greeted:
        pl.semaphore_signal(
            barrier, inc=1, device_id=peer, device_id_type=pl.DeviceIdType.MESH
        )

    def send(src, dst, sems, peer):
        copy = pltpu.make_async_remote_copy(
            src_ref=src,
            dst_ref=dst,
            send_sem=sems[0],
            recv_sem=sems[1],
            device_id=peer,
            device_id_type=pl.DeviceIdType.MESH,
        )
        copy.start()
        return copy

    def iota(shape, dim):
        return lax.broadcasted_iota(jnp.int32, shape, dim)

    def roll(values, shift, axis):
        return pltpu.roll(values, shift, axis)

    levels = (level0, level1, level2)
    halo_refs = (
        (first_send0, first_recv0, second_send0, second_recv0, halo_sems0),
        (first_send1, first_recv1, second_send1, second_recv1, halo_sems1),
        (first_send2, first_recv2, second_send2, second_recv2, halo_sems2),
    )
    used = [0, 0, 0]

    shape = (N, N, LANES)
    last_first = (iota(shape, 0) == N - 1) & (gx == gx_count - 1)
    last_second = (iota(shape, 1) == N - 1) & (gy == gy_count - 1)
    last_third = iota(shape, 2) == LANES - 1
    face_first = jnp.where(last_first, 0.0, diffuse_first[...])
    face_second = jnp.where(last_second, 0.0, diffuse_second[...])
    face_third = jnp.where(last_third, 0.0, diffuse_third[...])
    level0[FF] = face_first
    level0[FS] = face_second
    level0[FT] = face_third
    level0[LT] = roll(face_third, 1, 2)
    face_send[0] = face_first[N - 1]
    face_send[1] = face_second[:, N - 1, :]
    basis = deflation[...]
    basis_second_send[0] = basis[:, :, 0, :]
    basis_second_send[1] = basis[:, :, N - 1, :]

    pl.semaphore_wait(barrier, len(greeted))

    def setup_pair(place):
        return setup_sems.at[0, place], setup_sems.at[1, place]

    setup_copies = [
        send(face_send.at[0], face_recv.at[0], setup_pair(0), (gx_next, gy)),
        send(face_send.at[1], face_recv.at[1], setup_pair(1), (gx, gy_next)),
        send(basis_second_send.at[0], basis_second_recv.at[1], setup_pair(2), (gx, gy_prev)),
        send(basis_second_send.at[1], basis_second_recv.at[0], setup_pair(3), (gx, gy_next)),
        send(deflation.at[:, 0], basis_first_recv.at[1], setup_pair(4), (gx_prev, gy)),
        send(deflation.at[:, N - 1], basis_first_recv.at[0], setup_pair(5), (gx_next, gy)),
    ]
    setup_copies[0].wait()
    setup_copies[1].wait()
    row0 = iota(shape, 1)
    lower_first = jnp.concatenate([face_recv[0][None], face_first[: N - 1]], axis=0)
    lower_second = jnp.where(row0 == 0, face_recv[1][:, None, :], roll(face_second, 1, 1))
    level0[LF] = lower_first
    level0[LS] = lower_second

    def finish_level(level, react):
        diag = react + level[FF] + level[LF] + level[FS] + level[LS] + level[FT] + level[LT]
        level[DIAG] = diag
        level[INV] = 1.0 / diag

    finish_level(level0, reaction[...])

    def partner_up(values, step, axis):
        return roll(values, values.shape[axis] - step, axis)

    def halves(values, step, axis):
        even = lax.rem(iota(values.shape, axis) // step, 2) == 0
        return (
            jnp.where(even, values, roll(values, step, axis)),
            jnp.where(even, partner_up(values, step, axis), values),
        )

    def fold(values, step, axis):
        if axis == 0:
            pairs = values.reshape((values.shape[0] // 2, 2) + values.shape[1:])
            return pairs[:, 0] + pairs[:, 1]
        even, odd = halves(values, step, axis)
        return even + odd

    def first_half(values, which):
        pairs = values.reshape((values.shape[0] // 2, 2) + values.shape[1:])
        return pairs[:, which]

    def fold_block(values, step):
        return fold(fold(fold(values, step, 0), step, 1), step, 2)

    def coarsen(fine, coarse, react, step):
        coarse[FF] = fold(fold(first_half(fine[FF], 1), step, 1), step, 2)
        coarse[LF] = fold(fold(first_half(fine[LF], 0), step, 1), step, 2)
        coarse[FS] = halves(fold(fold(fine[FS], step, 0), step, 2), step, 1)[1]
        coarse[LS] = halves(fold(fold(fine[LS], step, 0), step, 2), step, 1)[0]
        coarse[FT] = halves(fold(fold(fine[FT], step, 0), step, 1), step, 2)[1]
        coarse[LT] = halves(fold(fold(fine[LT], step, 0), step, 1), step, 2)[0]
        react = fold_block(react, step)
        finish_level(coarse, react)
        return react

    react1 = coarsen(level0, level1, reaction[...], 1)
    coarsen(level1, level2, react1, 2)

    def inner_part(field, level, step):
        return (
            level[DIAG] * field
            - level[FT] * partner_up(field, step, 2)
            - level[LT] * roll(field, step, 2)
        )

    def outer_part(partial, field, level, step, first_lo, first_hi, second_lo, second_hi):
        row = iota(field.shape, 1)
        upper = jnp.where(row >= N - step, second_hi[:, None, :], partner_up(field, step, 1))
        lower = jnp.where(row < step, second_lo[:, None, :], roll(field, step, 1))
        if field.shape[0] > 1:
            after = jnp.concatenate([field[1:], first_hi[None]], axis=0)
            before = jnp.concatenate([first_lo[None], field[:-1]], axis=0)
        return (
            partial
            - level[FF] * after
            - level[LF] * before
            - level[FS] * upper
            - level[LS] * lower
        )

    mate_first = gx + 1 - 2 * lax.rem(gx, 2)
    mate_second = gy + 1 - 2 * lax.rem(gy, 2)
    starts, ends = gx == 0, gx == gx_count - 1
    opens, closes = gy == 0, gy == gy_count - 1
    peers = (
        (jnp.where(starts, gx, gx_prev), jnp.where(starts, mate_second, gy)),
        (jnp.where(ends, gx, gx_next), jnp.where(ends, mate_second, gy)),
        (jnp.where(opens, mate_first, gx), jnp.where(opens, gy, gy_prev)),
        (jnp.where(closes, mate_first, gx), jnp.where(closes, gy, gy_next)),
    )
    slots = tuple(
        jnp.where(at, other, slot).astype(jnp.int32)
        for at, other, slot in ((starts, 0, 1), (ends, 1, 0), (opens, 0, 1), (closes, 1, 0))
    )

    def operate(field, which, meanwhile=lambda: None):
        level = levels[which]
        step = 2**which
        first_send, first_recv, second_send, second_recv, sems = halo_refs[which]
        use = used[which]
        used[which] += 1
        cells = field.shape[0]
        first_send[use, 0] = field[0]
        first_send[use, 1] = field[cells - 1]
        second_send[use, 0] = field[:, 0, :]
        second_send[use, 1] = field[:, N - 1, :]

        def pair(place):
            return sems.at[0, use, place], sems.at[1, use, place]

        copies = []
        for place, (edge, slot, peer) in enumerate(
            (
                (first_send.at[use, 0], slots[0], peers[0]),
                (first_send.at[use, 1], slots[1], peers[1]),
                (second_send.at[use, 0], slots[2], peers[2]),
                (second_send.at[use, 1], slots[3], peers[3]),
            )
        ):
            first = place < 2
            landing = (first_recv if first else second_recv).at[use, slot]
            arrival = slot if first else slot + 2
            pair = sems.at[0, use, place], sems.at[1, use, arrival]
            copies.append(send(edge, landing, pair, peer))
        partial = inner_part(field, level, step)
        meanwhile()
        for place in range(4):
            copies[place].wait_send()
            landing = (first_recv if place < 2 else second_recv).at[use, place % 2]
            pltpu.make_async_remote_copy(
                src_ref=landing,
                dst_ref=landing,
                send_sem=sems.at[0, use, place],
                recv_sem=sems.at[1, use, place],
                device_id=peers[place],
                device_id_type=pl.DeviceIdType.MESH,
            ).wait_recv()
        return outer_part(
            partial,
            field,
            level,
            step,
            first_recv[use, 0],
            first_recv[use, 1],
            second_recv[use, 0],
            second_recv[use, 1],
        )

    def prolong_first(values):
        cells = values.shape[0]
        pairs = jnp.broadcast_to(values[:, None], (cells, 2) + values.shape[1:])
        return pairs.reshape((2 * cells,) + values.shape[1:])

    def cycle(right, which):
        level = levels[which]
        field = RELAX_WEIGHT * right * level[INV]
        if which == LEVELS - 1:
            for _ in range(COARSE_SWEEPS - 1):
                field = field + RELAX_WEIGHT * (right - operate(field, which)) * level[INV]
            return field
        defect = right - operate(field, which)
        field = field + prolong_first(cycle(fold_block(defect, 2**which), which + 1))
        return field + RELAX_WEIGHT * (right - operate(field, which)) * level[INV]

    summed = [0]

    def sum_devices(row):
        use = summed[0]
        summed[0] += 1
        place = 0
        for buffer, peers, mine in (
            (gather_second, second_peers, gy),
            (gather_first, first_peers, gx),
        ):
            slot = buffer.at[use, mine]
            slot[...] = row
            copies = []
            for peer in peers:
                sems = sum_sems.at[0, use, place], sum_sems.at[1, use, place]
                copies.append(send(slot, slot, sems, peer))
                place += 1
            for copy in copies:
                copy.wait()
            row = jnp.sum(buffer[use], axis=0)
        return row

    tile_shape = (8, LANES)
    lane = iota(tile_shape, 1)
    sub = iota(tile_shape, 0)

    def parts(fields):
        gathered = jnp.zeros(tile_shape, jnp.float32)
        for i, field in enumerate(fields):
            part = jnp.sum(field, axis=0)
            part = jnp.sum(part[:8] + part[8:], axis=0, keepdims=True)
            gathered = jnp.where(sub == i, part, gathered)
        return jnp.sum(gathered, axis=1, keepdims=True)

    def project(vectors, field):
        return parts(vectors[i] * field for i in range(BASIS))

    def pick(row, places):
        return jnp.sum(jnp.where(lane == places, row, 0.0), axis=1, keepdims=True)

    for copy in setup_copies[2:]:
        copy.wait()

    def image_step(j, tile):
        vector = deflation[j]
        image = outer_part(
            inner_part(vector, level0, 1),
            vector,
            level0,
            1,
            basis_first_recv[0, j],
            basis_first_recv[1, j],
            basis_second_recv[0, j],
            basis_second_recv[1, j],
        )
        images[j] = image
        return jnp.where(lane == j * BASIS + sub, project(deflation, image), tile)

    tile = lax.fori_loop(0, BASIS, image_step, jnp.zeros(tile_shape, jnp.float32))
    tile = jnp.where(
        lane == BASIS * BASIS + sub, project(deflation, source[...]), tile
    )
    row = sum_devices(jnp.sum(tile, axis=0, keepdims=True))

    def column(values, place):
        return jnp.sum(jnp.where(lane == place, values, 0.0), axis=1, keepdims=True)

    projections = pick(row, BASIS * BASIS + sub)
    work = jnp.where(lane - 2 * BASIS == sub, 1.0, 0.0)
    for j in range(BASIS):
        both = 0.5 * (pick(row, BASIS * j + sub) + pick(row, BASIS * sub + j))
        work = jnp.where(lane == j, both, work)
    for k in range(BASIS):
        col = column(work, k)
        pivot = col[k : k + 1]
        scaled = work[k : k + 1] / pivot
        work = jnp.where(sub == k, scaled, work - col * scaled)
    inverse_columns = [column(work, 2 * BASIS + i) for i in range(BASIS)]

    def solve(values):
        return [
            jnp.sum(
                jnp.broadcast_to(inverse_columns[i], tile_shape) * values,
                axis=0,
                keepdims=True,
            )[None]
            for i in range(BASIS)
        ]

    def expand(vectors, weights):
        out = weights[0] * vectors[0]
        for i in range(1, BASIS):
            out = out + weights[i] * vectors[i]
        return out

    weights = solve(jnp.broadcast_to(projections, tile_shape))
    iterate_out[...] = expand(deflation, weights)
    residual_out[...] = source[...] - expand(images, weights)

    inner_now = curve = None
    for turn in range(ITERS):
        residual = residual_out[...]
        precond = cycle(residual, 0)
        held = []

        def products():
            held.append(project(images, precond))
            held.append(residual * precond)
            if turn > 0:
                held.append(precond * image_kept[...])

        image = operate(precond, 0, products)
        scalars = parts([precond * image] + held[1:])
        tile = jnp.where(lane == sub, held[0], 0.0)
        tile = jnp.where(lane == BASIS + sub, scalars, tile)
        row = sum_devices(jnp.sum(tile, axis=0, keepdims=True))
        projected = jnp.broadcast_to(pick(row, sub), tile_shape)
        curve_next, inner_next, cross = [
            jnp.broadcast_to(pick(row, BASIS + i)[:1], (1, LANES))[None] for i in range(3)
        ]
        weights = solve(projected)
        for i in range(BASIS):
            curve_next = curve_next - weights[i] * projected[i : i + 1][None]
        direction = precond - expand(deflation, weights)
        image = image - expand(images, weights)
        if turn > 0:
            ratio = inner_next / inner_now
            direction = direction + ratio * search[...]
            image = image + ratio * image_kept[...]
            curve_next = curve_next + ratio * (ratio * curve + 2.0 * cross)
        inner_now, curve = inner_next, curve_next
        alpha = inner_now / curve
        iterate_out[...] = iterate_out[...] + alpha * direction
        residual_out[...] = residual_out[...] - alpha * image
        if turn + 1 < ITERS:
            search[...] = direction
            image_kept[...] = image


def per_device(sizes, *args):
    gx_count, gy_count = sizes
    vmem = lambda *shape: pltpu.VMEM(shape, jnp.float32)
    scratch = [
        vmem(8, N, N, LANES),
        vmem(8, N // 2, N, LANES),
        vmem(8, N // 4, N, LANES),
        vmem(BASIS, N, N, LANES),
        vmem(N, N, LANES),
        vmem(N, N, LANES),
        vmem(2, N, LANES),
        vmem(2, N, LANES),
        vmem(2, BASIS, N, LANES),
        vmem(2, BASIS, N, LANES),
        vmem(2, BASIS, N, LANES),
    ]
    for which, count in enumerate(EXCHANGES):
        scratch += [vmem(count, 2, N, LANES)] * 2 + [vmem(count, 2, N // 2**which, LANES)] * 2
    peers = gy_count - 1 + gx_count - 1
    scratch += [
        vmem(SUMS, gy_count, 1, LANES),
        vmem(SUMS, gx_count, 1, LANES),
        pltpu.SemaphoreType.DMA((2, 6)),
        pltpu.SemaphoreType.DMA((2, FINE_EXCHANGES, 4)),
        pltpu.SemaphoreType.DMA((2, MID_EXCHANGES, 4)),
        pltpu.SemaphoreType.DMA((2, COARSE_EXCHANGES, 4)),
        pltpu.SemaphoreType.DMA((2, SUMS, peers)),
    ]
    block = jax.ShapeDtypeStruct((N, N, LANES), jnp.float32)
    return pl.pallas_call(
        functools.partial(kernel, sizes),
        out_shape=(block, block),
        in_specs=[pl.BlockSpec(memory_space=pltpu.VMEM)] * 6,
        out_specs=(pl.BlockSpec(memory_space=pltpu.VMEM),) * 2,
        scratch_shapes=scratch,
        compiler_params=pltpu.CompilerParams(
            collective_id=0, has_side_effects=True, vmem_limit_bytes=48 * 1024 * 1024
        ),
        name="deflated_cg",
    )(*args)


def solution(mesh):
    sizes = (mesh.shape["gx"], mesh.shape["gy"])
    field = P("gx", "gy", None)
    return jax.shard_map(
        functools.partial(per_device, sizes),
        mesh=mesh,
        in_specs=(field, field, field, field, field, P(None, "gx", "gy", None)),
        out_specs=(field, field),
        check_vma=False,
    )
```

```python
import functools

import jax
import jax.numpy as jnp
from jax import lax
from jax.experimental import pallas as pl
from jax.experimental.pallas import tpu as pltpu
from jax.sharding import PartitionSpec as P

LEVELS = 3
COARSE_SWEEPS = 3
ITERS = 2
BASIS = 8
RELAX_WEIGHT = 0.6

N = 16
LANES = 128
SUMS = ITERS + 1
CYCLES = ITERS
FINE_EXCHANGES = 2 * CYCLES + ITERS
MID_EXCHANGES = 2 * CYCLES
COARSE_EXCHANGES = (COARSE_SWEEPS - 1) * CYCLES
EXCHANGES = (FINE_EXCHANGES, MID_EXCHANGES, COARSE_EXCHANGES)

FF, LF, FS, LS, FT, LT, DIAG, INV = range(8)


def kernel(
    sizes,
    source,
    diffuse_first,
    diffuse_second,
    diffuse_third,
    reaction,
    deflation,
    iterate_out,
    residual_out,
    level0,
    level1,
    level2,
    images,
    search,
    image_kept,
    face_send,
    face_recv,
    basis_second_send,
    basis_first_recv,
    basis_second_recv,
    first_send0,
    first_recv0,
    second_send0,
    second_recv0,
    first_send1,
    first_recv1,
    second_send1,
    second_recv1,
    first_send2,
    first_recv2,
    second_send2,
    second_recv2,
    gather_second,
    gather_first,
    setup_sems,
    halo_sems0,
    halo_sems1,
    halo_sems2,
    sum_sems,
):
    gx_count, gy_count = sizes
    gx = lax.axis_index("gx")
    gy = lax.axis_index("gy")
    gx_next, gx_prev = lax.rem(gx + 1, gx_count), lax.rem(gx + gx_count - 1, gx_count)
    gy_next, gy_prev = lax.rem(gy + 1, gy_count), lax.rem(gy + gy_count - 1, gy_count)

    second_peers = [(gx, lax.rem(gy + d, gy_count)) for d in range(1, gy_count)]
    first_peers = [(lax.rem(gx + d, gx_count), gy) for d in range(1, gx_count)]

    barrier = pltpu.get_barrier_semaphore()
    greeted = second_peers + first_peers
    for peer in greeted:
        pl.semaphore_signal(
            barrier, inc=1, device_id=peer, device_id_type=pl.DeviceIdType.MESH
        )

    def send(src, dst, sems, peer):
        copy = pltpu.make_async_remote_copy(
            src_ref=src,
            dst_ref=dst,
            send_sem=sems[0],
            recv_sem=sems[1],
            device_id=peer,
            device_id_type=pl.DeviceIdType.MESH,
        )
        copy.start()
        return copy

    def iota(shape, dim):
        return lax.broadcasted_iota(jnp.int32, shape, dim)

    def roll(values, shift, axis):
        return pltpu.roll(values, shift, axis)

    levels = (level0, level1, level2)
    halo_refs = (
        (first_send0, first_recv0, second_send0, second_recv0, halo_sems0),
        (first_send1, first_recv1, second_send1, second_recv1, halo_sems1),
        (first_send2, first_recv2, second_send2, second_recv2, halo_sems2),
    )
    used = [0, 0, 0]

    shape = (N, N, LANES)
    last_first = (iota(shape, 0) == N - 1) & (gx == gx_count - 1)
    last_second = (iota(shape, 1) == N - 1) & (gy == gy_count - 1)
    last_third = iota(shape, 2) == LANES - 1
    face_first = jnp.where(last_first, 0.0, diffuse_first[...])
    face_second = jnp.where(last_second, 0.0, diffuse_second[...])
    face_third = jnp.where(last_third, 0.0, diffuse_third[...])
    level0[FF] = face_first
    level0[FS] = face_second
    level0[FT] = face_third
    level0[LT] = roll(face_third, 1, 2)
    face_send[0] = face_first[N - 1]
    face_send[1] = face_second[:, N - 1, :]
    basis = deflation[...]
    basis_second_send[0] = basis[:, :, 0, :]
    basis_second_send[1] = basis[:, :, N - 1, :]

    pl.semaphore_wait(barrier, len(greeted))

    def setup_pair(place):
        return setup_sems.at[0, place], setup_sems.at[1, place]

    setup_copies = [
        send(face_send.at[0], face_recv.at[0], setup_pair(0), (gx_next, gy)),
        send(face_send.at[1], face_recv.at[1], setup_pair(1), (gx, gy_next)),
        send(basis_second_send.at[0], basis_second_recv.at[1], setup_pair(2), (gx, gy_prev)),
        send(basis_second_send.at[1], basis_second_recv.at[0], setup_pair(3), (gx, gy_next)),
        send(deflation.at[:, 0], basis_first_recv.at[1], setup_pair(4), (gx_prev, gy)),
        send(deflation.at[:, N - 1], basis_first_recv.at[0], setup_pair(5), (gx_next, gy)),
    ]
    setup_copies[0].wait()
    setup_copies[1].wait()
    row0 = iota(shape, 1)
    lower_first = jnp.concatenate([face_recv[0][None], face_first[: N - 1]], axis=0)
    lower_second = jnp.where(row0 == 0, face_recv[1][:, None, :], roll(face_second, 1, 1))
    level0[LF] = lower_first
    level0[LS] = lower_second

    def finish_level(level, react):
        diag = react + level[FF] + level[LF] + level[FS] + level[LS] + level[FT] + level[LT]
        level[DIAG] = diag

    finish_level(level0, reaction[...])

    def partner_up(values, step, axis):
        return roll(values, values.shape[axis] - step, axis)

    def halves(values, step, axis):
        even = lax.rem(iota(values.shape, axis) // step, 2) == 0
        return (
            jnp.where(even, values, roll(values, step, axis)),
            jnp.where(even, partner_up(values, step, axis), values),
        )

    def fold(values, step, axis):
        if axis == 0:
            pairs = values.reshape((values.shape[0] // 2, 2) + values.shape[1:])
            return pairs[:, 0] + pairs[:, 1]
        even, odd = halves(values, step, axis)
        return even + odd

    def first_half(values, which):
        pairs = values.reshape((values.shape[0] // 2, 2) + values.shape[1:])
        return pairs[:, which]

    def fold_block(values, step):
        return fold(fold(fold(values, step, 0), step, 1), step, 2)

    def coarsen(fine, coarse, react, step):
        coarse[FF] = fold(fold(first_half(fine[FF], 1), step, 1), step, 2)
        coarse[LF] = fold(fold(first_half(fine[LF], 0), step, 1), step, 2)
        coarse[FS] = halves(fold(fold(fine[FS], step, 0), step, 2), step, 1)[1]
        coarse[LS] = halves(fold(fold(fine[LS], step, 0), step, 2), step, 1)[0]
        coarse[FT] = halves(fold(fold(fine[FT], step, 0), step, 1), step, 2)[1]
        coarse[LT] = halves(fold(fold(fine[LT], step, 0), step, 1), step, 2)[0]
        react = fold_block(react, step)
        finish_level(coarse, react)
        return react

    def coarsen_fine():
        level0[INV] = 1.0 / level0[DIAG]
        kept.append(coarsen(level0, level1, reaction[...], 1))

    def coarsen_mid():
        level1[INV] = 1.0 / level1[DIAG]
        coarsen(level1, level2, kept[0], 2)
        level2[INV] = 1.0 / level2[DIAG]

    kept = []

    def inner_part(field, level, step):
        row = iota(field.shape, 1)
        upper = jnp.where(row >= N - step, 0.0, partner_up(field, step, 1))
        lower = jnp.where(row < step, 0.0, roll(field, step, 1))
        nothing = jnp.zeros_like(field[:1])
        return (
            level[DIAG] * field
            - level[FT] * partner_up(field, step, 2)
            - level[LT] * roll(field, step, 2)
            - level[FS] * upper
            - level[LS] * lower
            - level[FF] * jnp.concatenate([field[1:], nothing], axis=0)
            - level[LF] * jnp.concatenate([nothing, field[:-1]], axis=0)
        )

    def outer_part(partial, level, step, first_lo, first_hi, second_lo, second_hi):
        cells = partial.shape[0]
        row = iota((cells, 8, LANES), 1)
        low, high = level[LS, :, :8], level[FS, :, 8:]
        low = jnp.where(row < step, low * second_lo[:, None, :], 0.0)
        high = jnp.where(row >= 8 - step, high * second_hi[:, None, :], 0.0)
        partial = jnp.concatenate([partial[:, :8] - low, partial[:, 8:] - high], axis=1)
        front = partial[0] - level[LF, 0] * first_lo
        back = partial[cells - 1] - level[FF, cells - 1] * first_hi
        return jnp.concatenate([front[None], partial[1 : cells - 1], back[None]], axis=0)

    def operate(field, which, meanwhile=lambda: None):
        level = levels[which]
        step = 2**which
        first_send, first_recv, second_send, second_recv, sems = halo_refs[which]
        use = used[which]
        used[which] += 1
        cells = field.shape[0]
        first_send[use, 0] = field[0]
        first_send[use, 1] = field[cells - 1]
        second_send[use, 0] = field[:, 0, :]
        second_send[use, 1] = field[:, N - 1, :]

        def pair(place):
            return sems.at[0, use, place], sems.at[1, use, place]

        copies = [
            send(first_send.at[use, 0], first_recv.at[use, 1], pair(0), (gx_prev, gy)),
            send(first_send.at[use, 1], first_recv.at[use, 0], pair(1), (gx_next, gy)),
            send(second_send.at[use, 0], second_recv.at[use, 1], pair(2), (gx, gy_prev)),
            send(second_send.at[use, 1], second_recv.at[use, 0], pair(3), (gx, gy_next)),
        ]
        partial = inner_part(field, level, step)
        meanwhile()
        for copy in copies:
            copy.wait()
        return outer_part(
            partial,
            level,
            step,
            first_recv[use, 0],
            first_recv[use, 1],
            second_recv[use, 0],
            second_recv[use, 1],
        )

    def prolong_first(values):
        cells = values.shape[0]
        pairs = jnp.broadcast_to(values[:, None], (cells, 2) + values.shape[1:])
        return pairs.reshape((2 * cells,) + values.shape[1:])

    def cycle(right, which):
        level = levels[which]
        field = RELAX_WEIGHT * right * level[INV]
        if which == LEVELS - 1:
            for _ in range(COARSE_SWEEPS - 1):
                field = field + RELAX_WEIGHT * (right - operate(field, which)) * level[INV]
            return field
        defect = right - operate(field, which)
        field = field + prolong_first(cycle(fold_block(defect, 2**which), which + 1))
        return field + RELAX_WEIGHT * (right - operate(field, which)) * level[INV]

    summed = [0]

    def sum_devices(row, meanwhile=(lambda: None, lambda: None)):
        use = summed[0]
        summed[0] += 1
        place = 0
        for buffer, peers, mine, work in (
            (gather_second, second_peers, gy, meanwhile[0]),
            (gather_first, first_peers, gx, meanwhile[1]),
        ):
            slot = buffer.at[use, mine]
            slot[...] = row
            copies = []
            for peer in peers:
                sems = sum_sems.at[0, use, place], sum_sems.at[1, use, place]
                copies.append(send(slot, slot, sems, peer))
                place += 1
            work()
            for copy in copies:
                copy.wait()
            row = jnp.sum(buffer[use], axis=0)
        return row

    tile_shape = (8, LANES)
    lane = iota(tile_shape, 1)
    sub = iota(tile_shape, 0)

    def parts(fields):
        gathered = jnp.zeros(tile_shape, jnp.float32)
        for i, field in enumerate(fields):
            part = jnp.sum(field, axis=0)
            part = jnp.sum(part[:8] + part[8:], axis=0, keepdims=True)
            gathered = jnp.where(sub == i, part, gathered)
        return jnp.sum(gathered, axis=1, keepdims=True)

    def project(vectors, field):
        return parts(vectors[i] * field for i in range(BASIS))

    def pick(row, places):
        return jnp.sum(jnp.where(lane == places, row, 0.0), axis=1, keepdims=True)

    source_parts = project(deflation, source[...])
    for copy in setup_copies[2:]:
        copy.wait()

    def image_step(j, tile):
        vector = deflation[j]
        image = outer_part(
            inner_part(vector, level0, 1),
            level0,
            1,
            basis_first_recv[0, j],
            basis_first_recv[1, j],
            basis_second_recv[0, j],
            basis_second_recv[1, j],
        )
        images[j] = image
        return jnp.where(lane == j * BASIS + sub, project(deflation, image), tile)

    tile = lax.fori_loop(0, BASIS, image_step, jnp.zeros(tile_shape, jnp.float32))
    tile = jnp.where(lane == BASIS * BASIS + sub, source_parts, tile)
    row = sum_devices(jnp.sum(tile, axis=0, keepdims=True), (coarsen_fine, coarsen_mid))

    def column(values, place):
        return jnp.sum(jnp.where(lane == place, values, 0.0), axis=1, keepdims=True)

    projections = pick(row, BASIS * BASIS + sub)
    work = jnp.where(lane - 2 * BASIS == sub, 1.0, 0.0)
    for j in range(BASIS):
        both = 0.5 * (pick(row, BASIS * j + sub) + pick(row, BASIS * sub + j))
        work = jnp.where(lane == j, both, work)
    for k in range(BASIS):
        col = column(work, k)
        pivot = col[k : k + 1]
        scaled = work[k : k + 1] / pivot
        work = jnp.where(sub == k, scaled, work - col * scaled)
    inverse_columns = [column(work, 2 * BASIS + i) for i in range(BASIS)]

    def solve(values):
        return [
            jnp.sum(
                jnp.broadcast_to(inverse_columns[i], tile_shape) * values,
                axis=0,
                keepdims=True,
            )[None]
            for i in range(BASIS)
        ]

    def expand(vectors, weights):
        out = weights[0] * vectors[0]
        for i in range(1, BASIS):
            out = out + weights[i] * vectors[i]
        return out

    weights = solve(jnp.broadcast_to(projections, tile_shape))
    iterate_out[...] = expand(deflation, weights)
    residual_out[...] = source[...] - expand(images, weights)

    inner_now = curve = None
    for turn in range(ITERS):
        residual = residual_out[...]
        precond = cycle(residual, 0)
        held = []

        def products():
            held.append(project(images, precond))
            held.append(residual * precond)
            if turn > 0:
                held.append(precond * image_kept[...])

        image = operate(precond, 0, products)
        scalars = parts([precond * image] + held[1:])
        tile = jnp.where(lane == sub, held[0], 0.0)
        tile = jnp.where(lane == BASIS + sub, scalars, tile)
        row = sum_devices(jnp.sum(tile, axis=0, keepdims=True))
        projected = jnp.broadcast_to(pick(row, sub), tile_shape)
        curve_next, inner_next, cross = [
            jnp.broadcast_to(pick(row, BASIS + i)[:1], (1, LANES))[None] for i in range(3)
        ]
        weights = solve(projected)
        for i in range(BASIS):
            curve_next = curve_next - weights[i] * projected[i : i + 1][None]
        direction = precond - expand(deflation, weights)
        image = image - expand(images, weights)
        if turn > 0:
            ratio = inner_next / inner_now
            direction = direction + ratio * search[...]
            image = image + ratio * image_kept[...]
            curve_next = curve_next + ratio * (ratio * curve + 2.0 * cross)
        inner_now, curve = inner_next, curve_next
        alpha = inner_now / curve
        iterate_out[...] = iterate_out[...] + alpha * direction
        residual_out[...] = residual_out[...] - alpha * image
        if turn + 1 < ITERS:
            search[...] = direction
            image_kept[...] = image


def per_device(sizes, *args):
    gx_count, gy_count = sizes
    vmem = lambda *shape: pltpu.VMEM(shape, jnp.float32)
    scratch = [
        vmem(8, N, N, LANES),
        vmem(8, N // 2, N, LANES),
        vmem(8, N // 4, N, LANES),
        vmem(BASIS, N, N, LANES),
        vmem(N, N, LANES),
        vmem(N, N, LANES),
        vmem(2, N, LANES),
        vmem(2, N, LANES),
        vmem(2, BASIS, N, LANES),
        vmem(2, BASIS, N, LANES),
        vmem(2, BASIS, N, LANES),
    ]
    for which, count in enumerate(EXCHANGES):
        scratch += [vmem(count, 2, N, LANES)] * 2 + [vmem(count, 2, N // 2**which, LANES)] * 2
    peers = gy_count - 1 + gx_count - 1
    scratch += [
        vmem(SUMS, gy_count, 1, LANES),
        vmem(SUMS, gx_count, 1, LANES),
        pltpu.SemaphoreType.DMA((2, 6)),
        pltpu.SemaphoreType.DMA((2, FINE_EXCHANGES, 4)),
        pltpu.SemaphoreType.DMA((2, MID_EXCHANGES, 4)),
        pltpu.SemaphoreType.DMA((2, COARSE_EXCHANGES, 4)),
        pltpu.SemaphoreType.DMA((2, SUMS, peers)),
    ]
    block = jax.ShapeDtypeStruct((N, N, LANES), jnp.float32)
    return pl.pallas_call(
        functools.partial(kernel, sizes),
        out_shape=(block, block),
        in_specs=[pl.BlockSpec(memory_space=pltpu.VMEM)] * 6,
        out_specs=(pl.BlockSpec(memory_space=pltpu.VMEM),) * 2,
        scratch_shapes=scratch,
        compiler_params=pltpu.CompilerParams(
            collective_id=0, has_side_effects=True, vmem_limit_bytes=48 * 1024 * 1024
        ),
        name="deflated_cg",
    )(*args)


def solution(mesh):
    sizes = (mesh.shape["gx"], mesh.shape["gy"])
    field = P("gx", "gy", None)
    return jax.shard_map(
        functools.partial(per_device, sizes),
        mesh=mesh,
        in_specs=(field, field, field, field, field, P(None, "gx", "gy", None)),
        out_specs=(field, field),
        check_vma=False,
    )
```

```python
import functools

import jax
import jax.numpy as jnp
from jax import lax
from jax.experimental import pallas as pl
from jax.experimental.pallas import tpu as pltpu
from jax.sharding import PartitionSpec as P

LEVELS = 3
COARSE_SWEEPS = 3
ITERS = 2
BASIS = 8
RELAX_WEIGHT = 0.6

N = 16
LANES = 128
SUMS = ITERS + 1
CYCLES = ITERS
FINE_EXCHANGES = 2 * CYCLES + ITERS
MID_EXCHANGES = 2 * CYCLES
COARSE_EXCHANGES = (COARSE_SWEEPS - 1) * CYCLES
EXCHANGES = (FINE_EXCHANGES, MID_EXCHANGES, COARSE_EXCHANGES)

FF, LF, FS, LS, FT, LT, DIAG, INV = range(8)


def kernel(
    sizes,
    source,
    diffuse_first,
    diffuse_second,
    diffuse_third,
    reaction,
    deflation,
    iterate_out,
    residual_out,
    level0,
    level1,
    level2,
    images,
    search,
    image_kept,
    face_send,
    face_recv,
    basis_second_send,
    basis_first_recv,
    basis_second_recv,
    first_send0,
    first_recv0,
    second_send0,
    second_recv0,
    first_send1,
    first_recv1,
    second_send1,
    second_recv1,
    first_send2,
    first_recv2,
    second_send2,
    second_recv2,
    gather_second,
    gather_first,
    setup_sems,
    halo_sems0,
    halo_sems1,
    halo_sems2,
    sum_sems,
):
    gx_count, gy_count = sizes
    gx = lax.axis_index("gx")
    gy = lax.axis_index("gy")
    gx_next, gx_prev = lax.rem(gx + 1, gx_count), lax.rem(gx + gx_count - 1, gx_count)
    gy_next, gy_prev = lax.rem(gy + 1, gy_count), lax.rem(gy + gy_count - 1, gy_count)

    second_peers = [(gx, lax.rem(gy + d, gy_count)) for d in range(1, gy_count)]
    first_peers = [(lax.rem(gx + d, gx_count), gy) for d in range(1, gx_count)]

    barrier = pltpu.get_barrier_semaphore()
    greeted = second_peers + first_peers
    for peer in greeted:
        pl.semaphore_signal(
            barrier, inc=1, device_id=peer, device_id_type=pl.DeviceIdType.MESH
        )

    sent = []

    def send(src, dst, sems, peer):
        copy = pltpu.make_async_remote_copy(
            src_ref=src,
            dst_ref=dst,
            send_sem=sems[0],
            recv_sem=sems[1],
            device_id=peer,
            device_id_type=pl.DeviceIdType.MESH,
        )
        copy.start()
        sent.append(copy)
        return copy

    def iota(shape, dim):
        return lax.broadcasted_iota(jnp.int32, shape, dim)

    def roll(values, shift, axis):
        return pltpu.roll(values, shift, axis)

    levels = (level0, level1, level2)
    halo_refs = (
        (first_send0, first_recv0, second_send0, second_recv0, halo_sems0),
        (first_send1, first_recv1, second_send1, second_recv1, halo_sems1),
        (first_send2, first_recv2, second_send2, second_recv2, halo_sems2),
    )
    used = [0, 0, 0]

    shape = (N, N, LANES)
    last_first = (iota(shape, 0) == N - 1) & (gx == gx_count - 1)
    last_second = (iota(shape, 1) == N - 1) & (gy == gy_count - 1)
    last_third = iota(shape, 2) == LANES - 1
    face_first = jnp.where(last_first, 0.0, diffuse_first[...])
    face_second = jnp.where(last_second, 0.0, diffuse_second[...])
    face_third = jnp.where(last_third, 0.0, diffuse_third[...])
    level0[FF] = face_first
    level0[FS] = face_second
    level0[FT] = face_third
    level0[LT] = roll(face_third, 1, 2)
    face_send[0] = face_first[N - 1]
    face_send[1] = face_second[:, N - 1, :]
    basis = deflation[...]
    basis_second_send[0] = basis[:, :, 0, :]
    basis_second_send[1] = basis[:, :, N - 1, :]

    pl.semaphore_wait(barrier, len(greeted))

    def setup_pair(place):
        return setup_sems.at[0, place], setup_sems.at[1, place]

    setup_copies = [
        send(face_send.at[0], face_recv.at[0], setup_pair(0), (gx_next, gy)),
        send(face_send.at[1], face_recv.at[1], setup_pair(1), (gx, gy_next)),
        send(basis_second_send.at[0], basis_second_recv.at[1], setup_pair(2), (gx, gy_prev)),
        send(basis_second_send.at[1], basis_second_recv.at[0], setup_pair(3), (gx, gy_next)),
        send(deflation.at[:, 0], basis_first_recv.at[1], setup_pair(4), (gx_prev, gy)),
        send(deflation.at[:, N - 1], basis_first_recv.at[0], setup_pair(5), (gx_next, gy)),
    ]
    setup_copies[0].wait_recv()
    setup_copies[1].wait_recv()
    row0 = iota(shape, 1)
    lower_first = jnp.concatenate([face_recv[0][None], face_first[: N - 1]], axis=0)
    lower_second = jnp.where(row0 == 0, face_recv[1][:, None, :], roll(face_second, 1, 1))
    level0[LF] = lower_first
    level0[LS] = lower_second

    def finish_level(level, react):
        diag = react + level[FF] + level[LF] + level[FS] + level[LS] + level[FT] + level[LT]
        level[DIAG] = diag

    finish_level(level0, reaction[...])

    def partner_up(values, step, axis):
        return roll(values, values.shape[axis] - step, axis)

    def halves(values, step, axis):
        even = lax.rem(iota(values.shape, axis) // step, 2) == 0
        return (
            jnp.where(even, values, roll(values, step, axis)),
            jnp.where(even, partner_up(values, step, axis), values),
        )

    def fold(values, step, axis):
        if axis == 0:
            pairs = values.reshape((values.shape[0] // 2, 2) + values.shape[1:])
            return pairs[:, 0] + pairs[:, 1]
        even, odd = halves(values, step, axis)
        return even + odd

    def first_half(values, which):
        pairs = values.reshape((values.shape[0] // 2, 2) + values.shape[1:])
        return pairs[:, which]

    def fold_block(values, step):
        return fold(fold(fold(values, step, 0), step, 1), step, 2)

    def coarsen(fine, coarse, react, step):
        coarse[FF] = fold(fold(first_half(fine[FF], 1), step, 1), step, 2)
        coarse[LF] = fold(fold(first_half(fine[LF], 0), step, 1), step, 2)
        coarse[FS] = halves(fold(fold(fine[FS], step, 0), step, 2), step, 1)[1]
        coarse[LS] = halves(fold(fold(fine[LS], step, 0), step, 2), step, 1)[0]
        coarse[FT] = halves(fold(fold(fine[FT], step, 0), step, 1), step, 2)[1]
        coarse[LT] = halves(fold(fold(fine[LT], step, 0), step, 1), step, 2)[0]
        react = fold_block(react, step)
        finish_level(coarse, react)
        return react

    def coarsen_fine():
        level0[INV] = 1.0 / level0[DIAG]
        kept.append(coarsen(level0, level1, reaction[...], 1))

    def coarsen_mid():
        level1[INV] = 1.0 / level1[DIAG]
        coarsen(level1, level2, kept[0], 2)
        level2[INV] = 1.0 / level2[DIAG]

    kept = []

    def inner_part(field, level, step):
        row = iota(field.shape, 1)
        upper = jnp.where(row >= N - step, 0.0, partner_up(field, step, 1))
        lower = jnp.where(row < step, 0.0, roll(field, step, 1))
        nothing = jnp.zeros_like(field[:1])
        return (
            level[DIAG] * field
            - level[FT] * partner_up(field, step, 2)
            - level[LT] * roll(field, step, 2)
            - level[FS] * upper
            - level[LS] * lower
            - level[FF] * jnp.concatenate([field[1:], nothing], axis=0)
            - level[LF] * jnp.concatenate([nothing, field[:-1]], axis=0)
        )

    def outer_part(partial, level, step, first_lo, first_hi, second_lo, second_hi):
        cells = partial.shape[0]
        row = iota((cells, 8, LANES), 1)
        low, high = level[LS, :, :8], level[FS, :, 8:]
        low = jnp.where(row < step, low * second_lo[:, None, :], 0.0)
        high = jnp.where(row >= 8 - step, high * second_hi[:, None, :], 0.0)
        partial = jnp.concatenate([partial[:, :8] - low, partial[:, 8:] - high], axis=1)
        front = partial[0] - level[LF, 0] * first_lo
        back = partial[cells - 1] - level[FF, cells - 1] * first_hi
        return jnp.concatenate([front[None], partial[1 : cells - 1], back[None]], axis=0)

    def operate(field, which, meanwhile=lambda: None):
        level = levels[which]
        step = 2**which
        first_send, first_recv, second_send, second_recv, sems = halo_refs[which]
        use = used[which]
        used[which] += 1
        cells = field.shape[0]
        first_send[use, 0] = field[0]
        first_send[use, 1] = field[cells - 1]
        second_send[use, 0] = field[:, 0, :]
        second_send[use, 1] = field[:, N - 1, :]

        def pair(place):
            return sems.at[0, use, place], sems.at[1, use, place]

        copies = [
            send(first_send.at[use, 0], first_recv.at[use, 1], pair(0), (gx_prev, gy)),
            send(first_send.at[use, 1], first_recv.at[use, 0], pair(1), (gx_next, gy)),
            send(second_send.at[use, 0], second_recv.at[use, 1], pair(2), (gx, gy_prev)),
            send(second_send.at[use, 1], second_recv.at[use, 0], pair(3), (gx, gy_next)),
        ]
        partial = inner_part(field, level, step)
        meanwhile()
        for copy in copies:
            copy.wait_recv()
        return outer_part(
            partial,
            level,
            step,
            first_recv[use, 0],
            first_recv[use, 1],
            second_recv[use, 0],
            second_recv[use, 1],
        )

    def prolong_first(values):
        cells = values.shape[0]
        pairs = jnp.broadcast_to(values[:, None], (cells, 2) + values.shape[1:])
        return pairs.reshape((2 * cells,) + values.shape[1:])

    def cycle(right, which):
        level = levels[which]
        field = RELAX_WEIGHT * right * level[INV]
        if which == LEVELS - 1:
            for _ in range(COARSE_SWEEPS - 1):
                field = field + RELAX_WEIGHT * (right - operate(field, which)) * level[INV]
            return field
        defect = right - operate(field, which)
        field = field + prolong_first(cycle(fold_block(defect, 2**which), which + 1))
        return field + RELAX_WEIGHT * (right - operate(field, which)) * level[INV]

    summed = [0]

    def sum_devices(row, meanwhile=(lambda: None, lambda: None)):
        use = summed[0]
        summed[0] += 1
        place = 0
        for buffer, peers, mine, work in (
            (gather_second, second_peers, gy, meanwhile[0]),
            (gather_first, first_peers, gx, meanwhile[1]),
        ):
            slot = buffer.at[use, mine]
            slot[...] = row
            copies = []
            for peer in peers:
                sems = sum_sems.at[0, use, place], sum_sems.at[1, use, place]
                copies.append(send(slot, slot, sems, peer))
                place += 1
            work()
            for copy in copies:
                copy.wait_recv()
            row = jnp.sum(buffer[use], axis=0)
        return row

    tile_shape = (8, LANES)
    lane = iota(tile_shape, 1)
    sub = iota(tile_shape, 0)

    def parts(fields):
        gathered = jnp.zeros(tile_shape, jnp.float32)
        for i, field in enumerate(fields):
            part = jnp.sum(field, axis=0)
            part = jnp.sum(part[:8] + part[8:], axis=0, keepdims=True)
            gathered = jnp.where(sub == i, part, gathered)
        return jnp.sum(gathered, axis=1, keepdims=True)

    def project(vectors, field):
        return parts(vectors[i] * field for i in range(BASIS))

    def pick(row, places):
        return jnp.sum(jnp.where(lane == places, row, 0.0), axis=1, keepdims=True)

    source_parts = project(deflation, source[...])
    for copy in setup_copies[2:]:
        copy.wait_recv()

    def image_step(j, tile):
        vector = deflation[j]
        image = outer_part(
            inner_part(vector, level0, 1),
            level0,
            1,
            basis_first_recv[0, j],
            basis_first_recv[1, j],
            basis_second_recv[0, j],
            basis_second_recv[1, j],
        )
        images[j] = image
        return jnp.where(lane == j * BASIS + sub, project(deflation, image), tile)

    tile = lax.fori_loop(0, BASIS, image_step, jnp.zeros(tile_shape, jnp.float32))
    tile = jnp.where(lane == BASIS * BASIS + sub, source_parts, tile)
    row = sum_devices(jnp.sum(tile, axis=0, keepdims=True), (coarsen_fine, coarsen_mid))

    def column(values, place):
        return jnp.sum(jnp.where(lane == place, values, 0.0), axis=1, keepdims=True)

    projections = pick(row, BASIS * BASIS + sub)
    work = jnp.where(lane - 2 * BASIS == sub, 1.0, 0.0)
    for j in range(BASIS):
        both = 0.5 * (pick(row, BASIS * j + sub) + pick(row, BASIS * sub + j))
        work = jnp.where(lane == j, both, work)
    for k in range(BASIS):
        col = column(work, k)
        pivot = col[k : k + 1]
        scaled = work[k : k + 1] / pivot
        work = jnp.where(sub == k, scaled, work - col * scaled)
    inverse_columns = [column(work, 2 * BASIS + i) for i in range(BASIS)]

    def solve(values):
        return [
            jnp.sum(
                jnp.broadcast_to(inverse_columns[i], tile_shape) * values,
                axis=0,
                keepdims=True,
            )[None]
            for i in range(BASIS)
        ]

    def expand(vectors, weights):
        out = weights[0] * vectors[0]
        for i in range(1, BASIS):
            out = out + weights[i] * vectors[i]
        return out

    weights = solve(jnp.broadcast_to(projections, tile_shape))
    iterate_out[...] = expand(deflation, weights)
    residual_out[...] = source[...] - expand(images, weights)

    inner_now = curve = None
    for turn in range(ITERS):
        residual = residual_out[...]
        precond = cycle(residual, 0)
        held = []

        def products():
            held.append(project(images, precond))
            held.append(residual * precond)
            if turn > 0:
                held.append(precond * image_kept[...])

        image = operate(precond, 0, products)
        scalars = parts([precond * image] + held[1:])
        tile = jnp.where(lane == sub, held[0], 0.0)
        tile = jnp.where(lane == BASIS + sub, scalars, tile)
        row = sum_devices(jnp.sum(tile, axis=0, keepdims=True))
        projected = jnp.broadcast_to(pick(row, sub), tile_shape)
        curve_next, inner_next, cross = [
            jnp.broadcast_to(pick(row, BASIS + i)[:1], (1, LANES))[None] for i in range(3)
        ]
        weights = solve(projected)
        for i in range(BASIS):
            curve_next = curve_next - weights[i] * projected[i : i + 1][None]
        direction = precond - expand(deflation, weights)
        image = image - expand(images, weights)
        if turn > 0:
            ratio = inner_next / inner_now
            direction = direction + ratio * search[...]
            image = image + ratio * image_kept[...]
            curve_next = curve_next + ratio * (ratio * curve + 2.0 * cross)
        inner_now, curve = inner_next, curve_next
        alpha = inner_now / curve
        iterate_out[...] = iterate_out[...] + alpha * direction
        residual_out[...] = residual_out[...] - alpha * image
        if turn + 1 < ITERS:
            search[...] = direction
            image_kept[...] = image

    for copy in sent:
        copy.wait_send()


def per_device(sizes, *args):
    gx_count, gy_count = sizes
    vmem = lambda *shape: pltpu.VMEM(shape, jnp.float32)
    scratch = [
        vmem(8, N, N, LANES),
        vmem(8, N // 2, N, LANES),
        vmem(8, N // 4, N, LANES),
        vmem(BASIS, N, N, LANES),
        vmem(N, N, LANES),
        vmem(N, N, LANES),
        vmem(2, N, LANES),
        vmem(2, N, LANES),
        vmem(2, BASIS, N, LANES),
        vmem(2, BASIS, N, LANES),
        vmem(2, BASIS, N, LANES),
    ]
    for which, count in enumerate(EXCHANGES):
        scratch += [vmem(count, 2, N, LANES)] * 2 + [vmem(count, 2, N // 2**which, LANES)] * 2
    peers = gy_count - 1 + gx_count - 1
    scratch += [
        vmem(SUMS, gy_count, 1, LANES),
        vmem(SUMS, gx_count, 1, LANES),
        pltpu.SemaphoreType.DMA((2, 6)),
        pltpu.SemaphoreType.DMA((2, FINE_EXCHANGES, 4)),
        pltpu.SemaphoreType.DMA((2, MID_EXCHANGES, 4)),
        pltpu.SemaphoreType.DMA((2, COARSE_EXCHANGES, 4)),
        pltpu.SemaphoreType.DMA((2, SUMS, peers)),
    ]
    block = jax.ShapeDtypeStruct((N, N, LANES), jnp.float32)
    return pl.pallas_call(
        functools.partial(kernel, sizes),
        out_shape=(block, block),
        in_specs=[pl.BlockSpec(memory_space=pltpu.VMEM)] * 6,
        out_specs=(pl.BlockSpec(memory_space=pltpu.VMEM),) * 2,
        scratch_shapes=scratch,
        compiler_params=pltpu.CompilerParams(
            collective_id=0, has_side_effects=True, vmem_limit_bytes=48 * 1024 * 1024
        ),
        name="deflated_cg",
    )(*args)


def solution(mesh):
    sizes = (mesh.shape["gx"], mesh.shape["gy"])
    field = P("gx", "gy", None)
    return jax.shard_map(
        functools.partial(per_device, sizes),
        mesh=mesh,
        in_specs=(field, field, field, field, field, P(None, "gx", "gy", None)),
        out_specs=(field, field),
        check_vma=False,
    )
```
